32 devices in a mesh: group: 2 (over y), seq: 4 (over x, core), neuron: 4 (over z).
Axes of the slice: x: 2, y: 2, z: 4, core: 2. Of those that a mesh axis runs over, the one named last changes fastest.
Arguments:
- tokens: bfloat16 [1024, 8192], P(('group', 'neuron'), 'seq'), parts along dimension 0, may hold values from -6 to 6
- block_ids: int32 [1024, 6], P(('group', 'neuron')), parts along dimension 0, may hold values from 0 to 27, all different within a row; in each aligned block of 128 rows (0 to 127, 128 to 255, ...) at most 35 rows name the same one
- block_order: int32 [28], replicated, may hold values from 0 to 27, each once
- gate_weight: bfloat16 [28, 8192, 128], P('neuron', 'seq'), may hold values from -0.0625 to 0.0625
- up_weight: bfloat16 [28, 8192, 128], P('neuron', 'seq'), may hold values from -0.0625 to 0.0625
- down_weight: bfloat16 [28, 128, 8192], P('neuron', None, 'seq'), may hold values from -0.21875 to 0.21875
Outputs:
- ffn_out: bfloat16 [1024, 8192], P(('group', 'neuron'), 'seq'), parts along dimension 0
The draws below stay inside these ranges and needn't reach their ends.
There are 2 independent parts, one for each index of `group`. The reference program is written for one: setup_inputs(seed, part) draws one part's arguments, and reference() takes and returns one part's arrays. A program takes and returns all parts, laid end to end along the dimension named above; an argument that names none is the same for every part. Nothing has to cross between parts.
Inputs may be any that keep to these rules, and one draw needn't show every extreme that they name: `block_ids`: each token names 6 different blocks; among the 128 rows of one device no block is named more than 35 times, and some block exactly 35 times. `block_order`: every block sits in exactly one slot.
All inputs are finite; a program needn't handle non-finite values.
Results may differ from the reference program's by a relative error of at most 0.0058.
Values may be sent and summed in bfloat16 or wider, within the bound.
No kernel may reach another device: no remote copies, remote signals or barrier semaphores. Data moves between devices by JAX's collectives and lax.ppermute only.
A program may use at most 128 MiB of HBM per device.

```python
import math
import jax
import jax.numpy as jnp
import numpy as np
from jax import lax

D = 8192
BW = 128
K = 6
TOK_DEV = 128
NBLK = 28
TOKENS = 512
CAP = 35
N_NEURON = 4


def level_of(key, shape, shards, least, high):
    def one(dim, shards_of):
        draws = jax.random.uniform(jax.random.fold_in(jax.random.fold_in(key, 6), dim), (shards_of,), jnp.float32, least / len(shards), high / len(shards))
        return jnp.repeat(jnp.exp(draws), shape[dim] // shards_of).reshape((-1,) + (1,) * (len(shape) - dim - 1))

    gain = one(*shards[0])
    for cut in shards[1:]:
        gain = gain * one(*cut)
    return gain


def shared_out(rng, own, number, rows, number_of, top, most, lean):
    sequence = jax.random.permutation(rng, number_of)
    packed, common = load_shares(number_of, rows * top, most, lean, True), load_shares(number_of, rows * top, most, lean, False)
    places = jnp.arange(number_of)

    def named(tallies, rotation):
        used = int((tallies > 0).sum())
        fixed = max(1, used // 4)
        shifted = fixed + (places - fixed + rotation * (used - fixed)) % max(1, number_of - fixed)
        return jnp.zeros((number_of,), jnp.int32).at[sequence[jnp.where(places < fixed, places, shifted)]].set(jnp.asarray(tallies, jnp.int32))

    tallies = jnp.where(number % 4 == 0, named(packed, number // 4), named(common, number - number // 4 - 1))
    mixed = jax.random.permutation(jax.random.fold_in(own, 3), number_of)
    source_of, taker = mixed[0:number_of // 2 * 2:2], mixed[1:number_of // 2 * 2:2]
    margin = jnp.minimum(tallies[source_of] - 1, most - tallies[taker]) // 2
    margin = jnp.where((source_of == sequence[0]) | (taker == sequence[0]) | (tallies[taker] == 0), 0, jnp.maximum(margin, 0))
    shifted = jax.random.randint(jax.random.fold_in(own, 4), (number_of // 2,), 0, 1 << 20) % (margin + 1)
    tallies = tallies.at[source_of].add(-shifted).at[taker].add(shifted)
    members = jnp.searchsorted(jnp.cumsum(tallies), jnp.arange(rows * top), side="right").astype(jnp.int32)
    table = members.reshape(top, rows).T
    table = table[jax.random.permutation(jax.random.fold_in(own, 1), rows)]
    rotation = jax.random.randint(jax.random.fold_in(own, 2), (rows, 1), 0, top)
    return jnp.take_along_axis(table, (jnp.arange(top)[None, :] + rotation) % top, axis=1)


def load_shares(count, total, bound, skew, full):
    weights = [(1 << 20) // math.isqrt(grade ** skew) + 1 for grade in range(1, count + 1)]
    largest = bound if full else min(bound, max(-(-total // count), total * weights[0] // sum(weights)))
    least = 1 if total - largest >= count - 1 else 0
    holding, spare = [largest] + [least] * (count - 1), total - largest - least * (count - 1)
    while spare > 0:
        free = [i for i in range(1, count) if holding[i] < largest] or [i for i in range(1, count) if holding[i] < bound]
        pool, budget = sum([weights[i] for i in free]), spare
        for i in free:
            addition = min(bound - holding[i], max(1, budget * weights[i] // pool), spare)
            holding[i] = holding[i] + addition
            spare = spare - addition
    return np.array(holding)


def normal_values(key, extent, deviation, most, cuts=(), kind=jnp.bfloat16):
    array = jax.random.normal(key, extent, jnp.float32) * deviation
    if len(cuts) > 0:
        array = level_of(key, extent, cuts, -0.22, 0.18) * array
    return jnp.clip(array, min=-most, max=most).astype(kind)


def setup_inputs(seed: int = 0, part: int = 0) -> dict:
    key_list = jax.random.split(jax.random.key(seed), 7)
    part_keys = jax.random.split(jax.random.fold_in(key_list[6], part), 7)
    tokens = normal_values(part_keys[0], (TOKENS, D), 1.0, 6.0, ((0, 4), (1, 4)))
    block_ids_keys = jax.random.split(jax.random.fold_in(part_keys[1], 1), TOKENS // TOK_DEV)
    block_ids_turns = jax.random.permutation(jax.random.fold_in(part_keys[1], 3), TOKENS // TOK_DEV)
    block_ids = jax.vmap(lambda own, number: shared_out(jax.random.fold_in(part_keys[1], 2), own, number, TOK_DEV, NBLK, K, CAP, 2))(block_ids_keys, block_ids_turns).reshape((TOKENS, K))
    block_order = jax.random.permutation(key_list[2], NBLK).astype(jnp.int32)
    gate_weight = normal_values(key_list[3], (NBLK, D, BW), D ** -0.5, 0.0625, ((0, 4), (1, 4)))
    up_weight = normal_values(key_list[4], (NBLK, D, BW), D ** -0.5, 0.0625, ((0, 4), (1, 4)))
    down_weight = normal_values(key_list[5], (NBLK, BW, D), (K * BW) ** -0.5, 0.21875, ((0, 4), (2, 4)))
    return {"tokens": tokens, "block_ids": block_ids, "block_order": block_order, "gate_weight": gate_weight, "up_weight": up_weight, "down_weight": down_weight}


def reference(tokens, block_ids, block_order, gate_weight, up_weight, down_weight):
    block_count = block_order.shape[0]
    slot_of = jnp.zeros((block_count,), jnp.int32).at[block_order].set(jnp.arange(block_count, dtype=jnp.int32))
    pair_slots = slot_of[block_ids].reshape(-1).astype(jnp.int32)
    pair_order = jnp.argsort(pair_slots, stable=True).astype(jnp.int32)
    block_load = jnp.bincount(pair_slots, length=block_count).astype(jnp.int32)
    block_start = (jnp.cumsum(block_load) - block_load).astype(jnp.int32)
    block_room = N_NEURON * CAP
    padded_order = jnp.concatenate([pair_order, jnp.zeros((block_room,), jnp.int32)])

    def one_block(carry, slot):
        pair_index = lax.dynamic_slice(padded_order, (block_start[slot],), (block_room,))
        in_use = jnp.arange(block_room, dtype=jnp.int32) < block_load[slot]
        token_row = (pair_index // K).astype(jnp.int32)
        picked = tokens[token_row]
        gate = jnp.dot(picked, gate_weight[slot], preferred_element_type=jnp.float32)
        upper = jnp.dot(picked, up_weight[slot], preferred_element_type=jnp.float32)
        hidden = (jax.nn.silu(gate) * upper).astype(jnp.bfloat16)
        partial_value = jnp.dot(hidden, down_weight[slot], preferred_element_type=jnp.float32).astype(jnp.bfloat16)
        partial_value = lax.optimization_barrier(partial_value).astype(jnp.float32)
        partial_value = jnp.where(in_use[:, None], partial_value, jnp.float32(0.0))
        return carry.at[token_row].add(partial_value), None

    start_sum = jnp.zeros(tokens.shape, jnp.float32)
    total, unused = lax.scan(one_block, start_sum, jnp.arange(block_count, dtype=jnp.int32))
    return total.astype(jnp.bfloat16)
```

```python
import functools

import jax
import jax.numpy as jnp
from jax import lax
from jax.experimental import pallas as pl
from jax.experimental.pallas import tpu as pltpu
from jax.sharding import PartitionSpec as P


F32 = jnp.float32
BF16 = jnp.bfloat16


def swap(value, axis, stride):
    size = lax.axis_size(axis)
    return lax.ppermute(value, axis, [(i, i ^ stride) for i in range(size)])


def gate_up_body(bit_ref, first_ref, second_ref, gate_ref, up_ref, keep_ref, send_ref):
    rows = first_ref.shape[0]
    width = gate_ref.shape[2]
    both = jnp.concatenate([first_ref[...], second_ref[...]], axis=0)
    weight = jnp.concatenate([gate_ref[0], up_ref[0]], axis=1)
    result = jnp.dot(both, weight, preferred_element_type=F32)
    lower = bit_ref[0] == 0
    keep = jnp.where(lower, result[:rows], result[rows:])
    send = jnp.where(lower, result[rows:], result[:rows])
    keep_ref[0] = keep[:, :width]
    keep_ref[1] = keep[:, width:]
    send_ref[0] = send[:, :width]
    send_ref[1] = send[:, width:]


def gate_up(bit, first, second, gate_weight, up_weight):
    rows, depth = first.shape
    blocks, _, width = gate_weight.shape
    whole = pl.BlockSpec((rows, depth), lambda b, bit: (0, 0))
    weight = pl.BlockSpec((1, depth, width), lambda b, bit: (b, 0, 0))
    out = pl.BlockSpec((2, rows, width), lambda b, bit: (0, 0, b))
    shape = jax.ShapeDtypeStruct((2, rows, blocks * width), F32)
    return pl.pallas_call(
        gate_up_body,
        grid_spec=pltpu.PrefetchScalarGridSpec(
            num_scalar_prefetch=1,
            grid=(blocks,),
            in_specs=[whole, whole, weight, weight],
            out_specs=[out, out],
        ),
        out_shape=[shape, shape],
        cost_estimate=pl.CostEstimate(
            flops=8 * rows * depth * width * blocks,
            bytes_accessed=4 * blocks * depth * width + 4 * rows * depth,
            transcendentals=0,
        ),
        name="gate_up",
    )(bit, first, second, gate_weight, up_weight)


def hidden_body(bit_ref, here_ref, mine_ref, other_ref, first_ref, second_ref, out_ref):
    ids = jnp.where(bit_ref[0] == 0, first_ref[...], second_ref[...])
    per_token = ids.shape[1]
    blocks = here_ref.shape[0]
    rows = ids.shape[0]
    width = out_ref.shape[1] // blocks
    named = [jnp.broadcast_to(ids[:, k : k + 1], (rows, width)) for k in range(per_token)]
    for b in range(blocks):
        columns = slice(b * width, (b + 1) * width)
        gate = mine_ref[0, :, columns] + other_ref[0, :, columns].astype(F32)
        up = mine_ref[1, :, columns] + other_ref[1, :, columns].astype(F32)
        active = named[0] == here_ref[b]
        for k in range(1, per_token):
            active = active | (named[k] == here_ref[b])
        value = gate / (1.0 + jnp.exp(-gate)) * up
        out_ref[:, columns] = jnp.where(active, value, 0.0).astype(out_ref.dtype)


def hidden_of(bit, here, mine, other, first_ids, second_ids):
    rows, columns = mine.shape[1:]
    spec = pl.BlockSpec(memory_space=pltpu.VMEM)
    scalar = pl.BlockSpec(memory_space=pltpu.SMEM)
    return pl.pallas_call(
        hidden_body,
        in_specs=[scalar, scalar, spec, spec, spec, spec],
        out_specs=spec,
        out_shape=jax.ShapeDtypeStruct((rows, columns), BF16),
        cost_estimate=pl.CostEstimate(
            flops=10 * rows * columns,
            bytes_accessed=20 * rows * columns,
            transcendentals=rows * columns,
        ),
        name="hidden",
    )(bit, here, mine, other, first_ids, second_ids)


def down_body(bit_ref, mine_ref, other_ref, weight_ref, first_ref, second_ref):
    rows = mine_ref.shape[0]
    mine, other = mine_ref[...], other_ref[...]
    lower = bit_ref[0] == 0
    both = jnp.concatenate([mine, other], axis=0)
    result = jnp.dot(both, weight_ref[...], preferred_element_type=F32)
    first = jnp.where(lower, result[:rows], result[rows:])
    second = jnp.where(lower, result[rows:], result[:rows])
    first_ref[...] = first.astype(first_ref.dtype)
    second_ref[...] = second.astype(second_ref.dtype)


def down(bit, mine, other, weight, tile=512):
    rows, inner = mine.shape
    columns = weight.shape[1]
    whole = pl.BlockSpec((rows, inner), lambda j, bit: (0, 0))
    out = pl.BlockSpec((rows, tile), lambda j, bit: (0, j))
    return pl.pallas_call(
        down_body,
        grid_spec=pltpu.PrefetchScalarGridSpec(
            num_scalar_prefetch=1,
            grid=(columns // tile,),
            in_specs=[whole, whole, pl.BlockSpec((inner, tile), lambda j, bit: (0, j))],
            out_specs=[out, out],
        ),
        out_shape=[
            jax.ShapeDtypeStruct((rows, columns), F32),
            jax.ShapeDtypeStruct((rows, columns), BF16),
        ],
        cost_estimate=pl.CostEstimate(
            flops=4 * rows * inner * columns,
            bytes_accessed=2 * inner * columns + 6 * rows * columns,
            transcendentals=0,
        ),
        name="down",
    )(bit, mine, other, weight)


def local(tokens, block_ids, block_order, gate_weight, up_weight, down_weight):
    owners = lax.axis_size("neuron")
    parties = lax.axis_size("seq")
    blocks_here = gate_weight.shape[0]
    rows = tokens.shape[0]
    half = owners // 2
    chunks = 2 if owners <= 4 else 1
    step = rows // chunks
    me = lax.axis_index("neuron")
    bit = (lax.axis_index("seq") & 1).astype(jnp.int32).reshape(1)
    here = lax.dynamic_slice(block_order, (me * blocks_here,), (blocks_here,))
    down_flat = down_weight.reshape(-1, down_weight.shape[2])

    def cut(value, c):
        return lax.slice_in_dim(value, c * step, (c + 1) * step, axis=0)

    piece = {(0, None): tokens}
    for c in range(chunks):
        piece[(half, c)] = swap(cut(tokens, c), "neuron", half)
    stride = half // 2
    while stride >= 1:
        for offset in range(0, half, 2 * stride):
            piece[(offset + stride, None)] = swap(piece[(offset, None)], "neuron", stride)
        stride //= 2
    names = {0: block_ids}
    for offset in range(1, owners):
        names[offset] = swap(block_ids, "neuron", offset)
    stride = half // 2
    while stride >= 1:
        for c in range(chunks):
            for offset in range(half, owners, 2 * stride):
                piece[(offset + stride, c)] = swap(piece[(offset, c)], "neuron", stride)
        stride //= 2

    batches = [(offset, None) for offset in range(0, half, 2)]
    for c in range(chunks):
        batches += [(offset, c) for offset in range(half, owners, 2)]

    share = {}
    for offset, c in batches:
        first, second = piece[(offset, c)], piece[(offset + 1, c)]
        ids = [names[offset], names[offset + 1]]
        if c is not None:
            ids = [cut(value, c) for value in ids]
        keep, send = gate_up(bit, first, second, gate_weight, up_weight)
        total = keep + swap(send, "seq", 1)
        stride = 2
        while stride < parties // 2:
            total = total + swap(total, "seq", stride)
            stride *= 2
        other = swap(total, "seq", stride)
        mine = hidden_of(bit, here, total, other, ids[0], ids[1])
        share[(offset, c)], share[(offset + 1, c)] = down(
            bit, mine, swap(mine, "seq", 1), down_flat
        )

    stride = 1
    while stride < half:
        for c in [None] + list(range(chunks)):
            span = range(0, half, 2 * stride) if c is None else range(half, owners, 2 * stride)
            for offset in span:
                came = swap(share[(offset + stride, c)].astype(BF16), "neuron", stride)
                share[(offset, c)] = share[(offset, c)].astype(F32) + came.astype(F32)
        stride *= 2
    parts = []
    for c in range(chunks):
        came = swap(share[(half, c)].astype(BF16), "neuron", half)
        parts.append(cut(share[(0, None)], c).astype(F32) + came.astype(F32))
    return jnp.concatenate(parts, axis=0).astype(BF16)


def solution(mesh):
    return jax.shard_map(
        local,
        mesh=mesh,
        in_specs=(
            P(("group", "neuron"), "seq"),
            P(("group", "neuron"), None),
            P(),
            P("neuron", "seq", None),
            P("neuron", "seq", None),
            P("neuron", None, "seq"),
        ),
        out_specs=P(("group", "neuron"), "seq"),
        check_vma=False,
    )
```
